128 devices in a mesh: dp: 8 (over x_hi, y), expert: 16 (over z, x_lo, core).
Axes of the slice: x: 4 (x_hi: 2, x_lo: 2; x = x_hi * 2 + x_lo), y: 4, z: 4, core: 2. Of those that a mesh axis runs over, the one named last changes fastest.
Arguments:
- tokens: bfloat16 [32768, 5120], P(('dp', 'expert')), may hold values from -6 to 6
- cotangent: bfloat16 [32768, 5120], P(('dp', 'expert')), may hold values from -6 to 6
- slot_token: int32 [128, 16, 8], P(('dp', 'expert')), may hold values from 0 to 255, as said below
- slot_weight: float32 [128, 16, 8], P(('dp', 'expert')), may hold values from 0.1 to 1
- w_gate: bfloat16 [16, 5120, 1536], P('expert', None, 'dp'), may hold values from -0.078125 to 0.078125
- w_up: bfloat16 [16, 5120, 1536], P('expert', None, 'dp'), may hold values from -0.078125 to 0.078125
- w_down: bfloat16 [16, 1536, 5120], P('expert', 'dp'), may hold values from -0.15625 to 0.15625
Outputs:
- moe_out: bfloat16 [32768, 5120], P(('dp', 'expert'))
- grad_tokens: bfloat16 [32768, 5120], P(('dp', 'expert'))
- grad_gate: bfloat16 [16, 5120, 1536], P('expert', None, 'dp')
- grad_up: bfloat16 [16, 5120, 1536], P('expert', None, 'dp')
- grad_down: bfloat16 [16, 1536, 5120], P('expert', 'dp')
The draws below stay inside these ranges and needn't reach their ends.
Inputs may be any that keep to these rules, and one draw needn't show every extreme that they name: `slot_token`: each of the 128 x 16 rows of 8 entries names distinct tokens of its source device.
All inputs are finite; a program needn't handle non-finite values.
Results may differ from the reference program's by a relative error of at most 0.017.
Values may be sent and summed in bfloat16 or wider, within the bound.
A program may use at most 192 MiB of HBM per device.

```python
import math
import jax
import jax.numpy as jnp
from jax import lax

D = 5120
FF = 1536
TOK_DEV = 256
SLOT = 8
EXPERTS = 16
SHARD = 192
SOURCES = 128
TOKENS = 32768
N_DP = 8
N_EXPERT = 16


def draw_slot_token(key, part):
    key_list = jax.random.split(key, SOURCES * EXPERTS)

    def one_row(one_key):
        return jax.random.permutation(one_key, TOK_DEV)[:SLOT]
    picked = jax.vmap(one_row)(key_list)
    return picked.reshape(SOURCES, EXPERTS, SLOT).astype(jnp.int32)


def levels(rng, dims, cuts, smallest, top_value):
    level, own = 1.0, jax.random.fold_in(rng, 6)
    for dim, blocks in cuts:
        draws = jnp.exp(jax.random.uniform(jax.random.fold_in(own, dim), (blocks,), jnp.float32, smallest / len(cuts), top_value / len(cuts)))
        level = level * jnp.repeat(draws, dims[dim] // blocks).reshape([-1 if axis == dim else 1 for axis in range(len(dims))])
    return level


def normal_values(rng, extent, spread, most, cuts=(), kind=jnp.bfloat16):
    level = levels(rng, extent, cuts, -0.22, 0.18) if cuts else 1.0
    drawn = jax.random.normal(rng, extent, jnp.float32) * spread * level
    return jnp.minimum(jnp.maximum(drawn, -most), most).astype(kind)


def setup_inputs(seed: int = 0) -> dict:
    seeds = jax.random.split(jax.random.key(seed), 8)
    tokens = normal_values(seeds[0], (TOKENS, D), 1.0, 6.0, ((0, 128),))
    cotangent = normal_values(seeds[1], (TOKENS, D), 1.0, 6.0, ((0, 128),))
    slot_token = draw_slot_token(jax.random.fold_in(seeds[7], 71), 0)
    slot_weight = jnp.clip(jnp.exp(math.log(1.0) - 2.3025851 * jax.random.uniform(seeds[3], (SOURCES, EXPERTS, SLOT), jnp.float32) ** levels(seeds[3], (SOURCES, EXPERTS, SLOT), ((0, 128),), -0.2, 0.2)), 0.1, 1.0)
    w_gate = normal_values(seeds[4], (EXPERTS, D, FF), D ** -0.5, 0.078125, ((0, 16), (2, 8)))
    w_up = normal_values(seeds[5], (EXPERTS, D, FF), D ** -0.5, 0.078125, ((0, 16), (2, 8)))
    w_down = normal_values(seeds[6], (EXPERTS, FF, D), FF ** -0.5, 0.15625, ((0, 16), (1, 8)))
    return {"tokens": tokens, "cotangent": cotangent, "slot_token": slot_token, "slot_weight": slot_weight, "w_gate": w_gate, "w_up": w_up, "w_down": w_down}


def silu_parts(pre_gate):
    sigma_value = jax.nn.sigmoid(pre_gate)
    return pre_gate * sigma_value, sigma_value * (1.0 + pre_gate * (1.0 - sigma_value))


def combine(chosen, scales, arrived):
    table_rows = (chosen[None, :] == jnp.arange(TOK_DEV, dtype=jnp.int32)[:, None]).astype(jnp.float32) * scales[None, :]
    return jnp.dot(table_rows, arrived.astype(jnp.float32), precision=lax.Precision.HIGHEST)


def take_block(source_block, positions):
    return jnp.take(source_block, positions, axis=0)


def pick_rows(grid, which):
    return jax.vmap(jax.vmap(take_block))(grid, which)


def reference(tokens, cotangent, slot_token, slot_weight, w_gate, w_up, w_down):
    groups = N_DP
    experts = N_EXPERT
    row_total = groups * experts * SLOT
    token_grid = tokens.reshape(groups, experts, TOK_DEV, D)
    grad_grid = cotangent.reshape(groups, experts, TOK_DEV, D)
    chosen = slot_token.reshape(groups, experts, experts, SLOT)
    scales = slot_weight.reshape(groups, experts, experts, SLOT)

    def per_expert(inputs):
        expert_id, weight_gate, weight_up, weight_down = inputs
        which = jnp.take(chosen, expert_id, axis=2)
        scale_now = jnp.take(scales, expert_id, axis=2)
        expert_rows = pick_rows(token_grid, which).reshape(row_total, D)
        out_grad = (pick_rows(grad_grid, which).astype(jnp.float32) * scale_now[..., None]).astype(jnp.bfloat16)
        out_grad = out_grad.reshape(row_total, D)
        gate_value = jnp.dot(expert_rows, weight_gate, preferred_element_type=jnp.float32)
        upward = jnp.dot(expert_rows, weight_up, preferred_element_type=jnp.float32)
        active, slope_term = silu_parts(gate_value)
        hidden = (active * upward).astype(jnp.bfloat16)
        hidden_shards = hidden.astype(jnp.float32).reshape(row_total, groups, SHARD)
        down_shards = weight_down.astype(jnp.float32).reshape(groups, SHARD, D)
        partial_value = jnp.einsum("rqf,qfd->qrd", hidden_shards, down_shards).astype(jnp.bfloat16)
        partial_value = lax.optimization_barrier(partial_value)
        expert_out = jnp.sum(partial_value.astype(jnp.float32), axis=0).astype(jnp.bfloat16)
        hidden_grad = jnp.dot(out_grad, weight_down.T, preferred_element_type=jnp.float32)
        gate_grad = (hidden_grad * upward * slope_term).astype(jnp.bfloat16)
        upward_grad = (hidden_grad * active).astype(jnp.bfloat16)
        grad_down = jnp.dot(hidden.T, out_grad, preferred_element_type=jnp.float32).astype(jnp.bfloat16)
        grad_gate = jnp.dot(expert_rows.T, gate_grad, preferred_element_type=jnp.float32).astype(jnp.bfloat16)
        grad_up = jnp.dot(expert_rows.T, upward_grad, preferred_element_type=jnp.float32).astype(jnp.bfloat16)
        gate_shards = gate_grad.astype(jnp.float32).reshape(row_total, groups, SHARD)
        upward_shards = upward_grad.astype(jnp.float32).reshape(row_total, groups, SHARD)
        gate_weights = weight_gate.astype(jnp.float32).reshape(D, groups, SHARD)
        upward_weights = weight_up.astype(jnp.float32).reshape(D, groups, SHARD)
        input_part = jnp.einsum("rqf,dqf->qrd", gate_shards, gate_weights) + jnp.einsum("rqf,dqf->qrd", upward_shards, upward_weights)
        input_part = lax.optimization_barrier(input_part.astype(jnp.bfloat16))
        input_grad = jnp.sum(input_part.astype(jnp.float32), axis=0).astype(jnp.bfloat16)
        return expert_out, input_grad, grad_gate, grad_up, grad_down

    expert_out, input_grad, grad_gate, grad_up, grad_down = lax.map(
        per_expert, (jnp.arange(experts, dtype=jnp.int32), w_gate, w_up, w_down))

    def to_sources(stacked):
        shaped = stacked.reshape(experts, groups, experts, SLOT, D)
        return shaped.transpose(1, 2, 0, 3, 4).reshape(groups * experts, experts * SLOT, D)

    flat_chosen = slot_token.reshape(groups * experts, experts * SLOT)
    flat_scales = slot_weight.reshape(groups * experts, experts * SLOT)
    unit_scales = jnp.ones_like(flat_scales)

    def merge_one(inputs):
        chosen_now, scales_now, arrived = inputs
        return combine(chosen_now, scales_now, arrived).astype(jnp.bfloat16)

    moe_out = lax.map(merge_one, (flat_chosen, flat_scales, to_sources(expert_out))).reshape(TOKENS, D)
    grad_tokens = lax.map(merge_one, (flat_chosen, unit_scales, to_sources(input_grad))).reshape(TOKENS, D)
    return moe_out, grad_tokens, grad_gate, grad_up, grad_down
```

```python
import jax
import jax.numpy as jnp
from jax import lax
from jax.sharding import PartitionSpec as P

AXES = ("dp", "expert")


def silu_parts(pre_gate):
    sigma_value = jax.nn.sigmoid(pre_gate)
    return (pre_gate * sigma_value, sigma_value * (1.0 + pre_gate * (1.0 - sigma_value)))


def combine(chosen, scales, arrived, token_count):
    table_rows = (chosen[None, :] == jnp.arange(token_count, dtype=jnp.int32)[:, None]).astype(
        jnp.float32
    ) * scales[None, :]
    return jnp.dot(table_rows, arrived.astype(jnp.float32), precision=lax.Precision.HIGHEST)


def plans(n_dp, n_expert):
    n_y = n_dp // 2
    across, rows, weights = [], [], []
    for d in range(n_dp):
        x_hi, y = d // n_y, d % n_y
        for e in range(n_expert):
            me = d * n_expert + e
            core = e % 2
            near = y ^ 1
            far = (((y + 1) ^ 1) - 1) % n_y
            weight_y, row_y = (near, far) if core == 0 else (far, near)
            across.append((me, ((1 - x_hi) * n_y + y) * n_expert + e))
            rows.append((me, (x_hi * n_y + row_y) * n_expert + e))
            weights.append((me, (x_hi * n_y + weight_y) * n_expert + e))
    return across, rows, weights


def exchange(value, plan):
    return lax.ppermute(value, AXES, plan)


def dot(left, right, contract):
    return lax.dot_general(
        left, right, (contract, ((), ())), preferred_element_type=jnp.float32
    )


NN = ((1,), (0,))
NT = ((1,), (1,))
TN = ((0,), (0,))


def on_device(tokens, cotangent, slot_token, slot_weight, w_gate, w_up, w_down):
    across, row_pairs, weight_pairs = plans(lax.axis_size("dp"), lax.axis_size("expert"))
    token_count = tokens.shape[0]
    chosen = slot_token.reshape(-1)
    scales = slot_weight.reshape(-1)
    gates = [w_gate[0], exchange(w_gate[0], weight_pairs)]
    ups = [w_up[0], exchange(w_up[0], weight_pairs)]
    downs = [w_down[0], exchange(w_down[0], weight_pairs)]
    sent_tokens = jnp.take(tokens, chosen, axis=0)
    sent_grads = (jnp.take(cotangent, chosen, axis=0).astype(jnp.float32) * scales[:, None]).astype(
        jnp.bfloat16
    )

    def spread(sent):
        landed = lax.all_to_all(sent, "expert", split_axis=0, concat_axis=0, tiled=True)
        two = jnp.concatenate([landed, exchange(landed, across)], axis=0)
        return [two, exchange(two, row_pairs)]

    def gather_back(parts):
        own, other = parts
        kept = own + exchange(other.astype(jnp.bfloat16), row_pairs).astype(jnp.float32)
        half = kept.shape[0] // 2
        away = exchange(kept[half:].astype(jnp.bfloat16), across)
        summed = (kept[:half] + away.astype(jnp.float32)).astype(jnp.bfloat16)
        return lax.all_to_all(summed, "expert", split_axis=0, concat_axis=0, tiled=True)

    token_rows = spread(sent_tokens)
    grad_rows = spread(sent_grads)
    token_all = jnp.concatenate(token_rows, axis=0)
    grad_all = jnp.concatenate(grad_rows, axis=0)
    half = token_all.shape[0] // 2
    hidden, gate_grad, upward_grad = [], [], []
    for s in range(2):
        gate_value = dot(token_all, gates[s], NN)
        upward = dot(token_all, ups[s], NN)
        active, slope_term = silu_parts(gate_value)
        hidden.append((active * upward).astype(jnp.bfloat16))
        hidden_grad = dot(grad_all, downs[s], NT)
        gate_grad.append((hidden_grad * upward * slope_term).astype(jnp.bfloat16))
        upward_grad.append((hidden_grad * active).astype(jnp.bfloat16))

    def out_part(rows):
        return dot(hidden[0][rows], downs[0], NN) + dot(hidden[1][rows], downs[1], NN)

    def input_part(rows):
        total = dot(gate_grad[0][rows], gates[0], NT) + dot(upward_grad[0][rows], ups[0], NT)
        return total + dot(gate_grad[1][rows], gates[1], NT) + dot(upward_grad[1][rows], ups[1], NT)

    first, second = slice(0, half), slice(half, 2 * half)
    returned = gather_back((out_part(first), out_part(second)))
    moe_out = combine(chosen, scales, returned, token_count).astype(jnp.bfloat16)
    returned_grad = gather_back((input_part(first), input_part(second)))
    grad_tokens = combine(chosen, jnp.ones_like(scales), returned_grad, token_count).astype(
        jnp.bfloat16
    )

    def weight_grad(of):
        away = exchange(of(1).astype(jnp.bfloat16), weight_pairs)
        return (of(0) + away.astype(jnp.float32)).astype(jnp.bfloat16)[None]

    grad_down = weight_grad(lambda s: dot(hidden[s], grad_all, TN))
    grad_gate = weight_grad(lambda s: dot(token_all, gate_grad[s], TN))
    grad_up = weight_grad(lambda s: dot(token_all, upward_grad[s], TN))
    return (moe_out, grad_tokens, grad_gate, grad_up, grad_down)


def solution(mesh):
    in_specs = (
        P(("dp", "expert"), None),
        P(("dp", "expert"), None),
        P(("dp", "expert"), None, None),
        P(("dp", "expert"), None, None),
        P("expert", None, "dp"),
        P("expert", None, "dp"),
        P("expert", "dp", None),
    )
    out_specs = (
        P(("dp", "expert"), None),
        P(("dp", "expert"), None),
        P("expert", None, "dp"),
        P("expert", None, "dp"),
        P("expert", "dp", None),
    )
    return jax.shard_map(
        on_device, mesh=mesh, in_specs=in_specs, out_specs=out_specs, check_vma=False
    )
```

```python
import functools

import jax
import jax.numpy as jnp
from jax import lax
from jax.experimental import pallas as pl
from jax.experimental.pallas import tpu as pltpu
from jax.sharding import PartitionSpec as P

MESH = pl.DeviceIdType.MESH
F32 = jnp.float32
BF16 = jnp.bfloat16
STEP = 512


def dot(left, right, left_dim=1, right_dim=0):
    return lax.dot_general(
        left, right, (((left_dim,), (right_dim,)), ((), ())), preferred_element_type=F32
    )


def over(count, body):
    lax.fori_loop(0, count, lambda i, carry: (body(i), carry)[1], 0)


def columns(index, width, base=0):
    return pl.ds(pl.multiple_of(base + index * width, 128), width)


def layer(
    sizes,
    chosen_ref,
    scale_ref,
    tokens,
    cotangent,
    w_gate,
    w_up,
    w_down,
    moe_out,
    grad_tokens,
    grad_gate,
    grad_up,
    grad_down,
    gates,
    ups,
    downs,
    token_rows,
    grad_rows,
    sent_tokens,
    sent_grads,
    part_out,
    part_in,
    first_a,
    first_b,
    second_a,
    second_b,
    back_out,
    back_in,
    swap_from,
    swap_to,
    acts_t,
    acts,
    pre,
    pre_down,
    send_sems,
    recv_sems,
    local_sems,
):
    n_dp, n_expert, slot = sizes
    n_y = n_dp // 2
    d = lax.axis_index("dp")
    e = lax.axis_index("expert")
    x_hi, y = d // n_y, d % n_y
    core = e % 2
    near = (1 - 2 * core) * (1 - 2 * (y % 2))
    side_x = ((1 - x_hi) * n_y + y, e)
    side_y = (x_hi * n_y + (y - near + n_y) % n_y, e)
    side_w = (x_hi * n_y + (y + near + n_y) % n_y, e)
    peers = [(d, (e + k) % n_expert) for k in range(1, n_expert)]
    width = tokens.shape[1]
    token_count = tokens.shape[0]
    block = n_expert * slot
    all_rows = 4 * block
    shard = w_down.shape[0]
    both = 2 * shard
    cut = first_a.shape[2]
    rest = width - cut
    part_a, part_b = pl.ds(0, cut), pl.ds(cut, rest)

    counter = [0]

    def remote(source, target, device):
        i = counter[0]
        counter[0] += 1
        return pltpu.make_async_remote_copy(
            src_ref=source,
            dst_ref=target,
            send_sem=send_sems.at[i],
            recv_sem=recv_sems.at[i],
            device_id=device,
            device_id_type=MESH,
        )

    local_counter = [0]

    def local(source, target):
        i = local_counter[0]
        local_counter[0] += 1
        copy = pltpu.make_async_copy(source, target, local_sems.at[i])
        copy.start()
        return copy

    take_tokens = local(tokens, swap_from.at[pl.ds(0, token_count)])
    take_cotangent = local(cotangent, swap_from.at[pl.ds(token_count, token_count)])
    weights = ((w_gate, gates), (w_up, ups), (w_down, downs))
    take_weights = [local(own, held.at[pl.ds(0, shard)]) for own, held in weights]

    barrier = pltpu.get_barrier_semaphore()
    partners = peers + [side_x, side_y, side_w]
    for partner in partners:
        pl.semaphore_signal(barrier, inc=1, device_id=partner, device_id_type=MESH)
    pl.semaphore_wait(barrier, len(partners))

    swaps = [remote(own, held.at[pl.ds(shard, shard)], side_w) for own, held in weights]
    for copy in swaps:
        copy.start()

    def all_to_all(source, target):
        copies = [
            remote(source.at[pl.ds(peer[1] * slot, slot)], target.at[pl.ds(e * slot, slot)], peer)
            for peer in peers
        ]
        for copy in copies:
            copy.start()
        mine = local(source.at[pl.ds(e * slot, slot)], target.at[pl.ds(e * slot, slot)])
        return copies, mine

    def landed(group):
        for copy in group[0]:
            copy.wait_recv()
        group[1].wait()

    def wait_sends(copies):
        for copy in copies:
            copy.wait_send()

    token_ids = lax.broadcasted_iota(jnp.int32, (token_count, block), 0)
    named = jnp.where(token_ids == chosen_ref[...], 1.0, 0.0).astype(F32)
    picks = jnp.transpose(named).astype(BF16)
    scale_column = jnp.transpose(jnp.broadcast_to(scale_ref[...], (block, block)))[:, :1]

    take_tokens.wait()

    def pick_tokens(i):
        at = columns(i, STEP)
        sent_tokens[:, at] = dot(picks, swap_from[pl.ds(0, token_count), at]).astype(BF16)

    over(width // STEP, pick_tokens)
    out_tokens = all_to_all(sent_tokens, token_rows)
    take_cotangent.wait()

    def pick_grads(i):
        at = columns(i, STEP)
        rows = dot(picks, swap_from[pl.ds(token_count, token_count), at])
        sent_grads[:, at] = (rows * scale_column).astype(BF16)

    over(width // STEP, pick_grads)
    out_grads = all_to_all(sent_grads, grad_rows)

    def block_of(i, n=1):
        return pl.ds(i * block, n * block)

    def spread(rows):
        to_x = remote(rows.at[block_of(0)], rows.at[block_of(1)], side_x)
        to_y = remote(rows.at[block_of(0)], rows.at[block_of(2)], side_y)
        on_y = remote(rows.at[block_of(1), part_a], rows.at[block_of(3), part_a], side_y)
        on_x = remote(rows.at[block_of(2), part_b], rows.at[block_of(3), part_b], side_x)
        return to_x, to_y, on_y, on_x

    def relay(group):
        to_x, to_y, on_y, on_x = group
        to_y.wait_recv()
        on_x.start()
        to_x.wait_recv()
        on_y.start()

    landed(out_tokens)
    token_spread = spread(token_rows)
    token_spread[0].start()
    token_spread[1].start()
    relay(token_spread)
    landed(out_grads)
    grad_spread = spread(grad_rows)
    grad_spread[0].start()
    grad_spread[1].start()

    deep = 2 * STEP

    def project(target, weight, side, rows):
        target[...] = jnp.zeros(target.shape, F32)

        def one(i):
            at = columns(i, deep)
            target[...] += dot(weight[pl.ds(side * shard, shard), at], rows[:, at], 1, 1)

        over(width // deep, one)

    for copy in take_weights:
        copy.wait()
    token_spread[2].wait_recv()
    token_spread[3].wait_recv()
    own, other = pl.ds(0, shard), pl.ds(shard, shard)
    project(pre.at[0, own], gates, 0, token_rows)
    project(pre.at[1, own], ups, 0, token_rows)
    swaps[0].wait_recv()
    project(pre.at[0, other], gates, 1, token_rows)
    swaps[1].wait_recv()
    project(pre.at[1, other], ups, 1, token_rows)

    def keep(which, at, value):
        acts_t[which, at] = value.astype(BF16)
        acts[which, :, at] = jnp.transpose(value).astype(BF16)

    for i in range(both // 128):
        at = pl.ds(i * 128, 128)
        gate_value = pre[0, at]
        keep(2, at, gate_value * jax.nn.sigmoid(gate_value) * pre[1, at])

    relay(grad_spread)

    def give(parts, terms, stream):
        def one(i):
            at = columns(i, STEP)
            total = dot(acts[terms[0][0]], terms[0][1][:, at])
            for which, weight in terms[1:]:
                total += dot(acts[which], weight[:, at])
            parts[:, at] = total.astype(BF16)

        over(cut // STEP, one)
        near_y = remote(parts.at[block_of(2, 2), part_a], first_a.at[stream], side_y)
        near_y.start()
        over(rest // STEP, lambda i: one(i + cut // STEP))
        me_x = remote(parts.at[block_of(1), part_b], first_b.at[stream, block_of(0)], side_x)
        far_x = remote(parts.at[block_of(3), part_b], first_b.at[stream, block_of(1)], side_x)
        me_x.start()
        far_x.start()
        return near_y, me_x, far_x

    def add_on(parts, near, stream):
        near_y, me_x, far_x = near
        near_y.wait_recv()

        def one(i):
            at = columns(i, STEP)
            total = parts[block_of(1), at].astype(F32) + first_a[stream, block_of(1), at].astype(F32)
            first_a[stream, block_of(1), at] = total.astype(BF16)

        over(cut // STEP, one)
        on_x = remote(first_a.at[stream, block_of(1)], second_a.at[stream], side_x)
        on_x.start()
        far_x.wait_recv()

        def two(i):
            at = columns(i, STEP)
            of = columns(i, STEP, cut)
            total = parts[block_of(2), of].astype(F32) + first_b[stream, block_of(1), at].astype(F32)
            first_b[stream, block_of(1), at] = total.astype(BF16)

        over(rest // STEP, two)
        on_y = remote(first_b.at[stream, block_of(1)], second_b.at[stream], side_y)
        on_y.start()
        me_x.wait_recv()
        return on_x, on_y

    def finish(parts, on, sums, stream):
        on_x, on_y = on
        on_x.wait_recv()

        def one(i):
            at = columns(i, STEP)
            total = parts[block_of(0), at].astype(F32) + first_a[stream, block_of(0), at].astype(F32)
            sums[:, at] = (total + second_a[stream, :, at].astype(F32)).astype(BF16)

        over(cut // STEP, one)
        on_y.wait_recv()

        def two(i):
            at = columns(i, STEP)
            of = columns(i, STEP, cut)
            total = parts[block_of(0), of].astype(F32) + first_b[stream, block_of(0), at].astype(F32)
            sums[:, of] = (total + second_b[stream, :, at].astype(F32)).astype(BF16)

        over(rest // STEP, two)

    swaps[2].wait_recv()
    near_out = give(part_out, [(2, downs)], 0)

    grad_spread[2].wait_recv()
    grad_spread[3].wait_recv()

    def slab(which):
        return pl.ds(which * shard, shard)

    def swap_grad(which, rows):
        def one(i):
            at = columns(i, STEP)
            swap_from[slab(which), at] = dot(acts_t[which, other], rows[:, at]).astype(BF16)

        over(width // STEP, one)
        copy = remote(swap_from.at[slab(which)], swap_to.at[slab(which)], side_w)
        copy.start()
        return copy

    def own_grad(which, rows, copy, target):
        copy.wait_recv()

        def one(i):
            at = columns(i, STEP)
            total = dot(acts_t[which, own], rows[:, at]) + swap_to[slab(which), at].astype(F32)
            swap_to[slab(which), at] = total.astype(BF16)

        over(width // STEP, one)
        return local(swap_to.at[slab(which)], target)

    swap_down = swap_grad(2, grad_rows)
    project(pre_down.at[own], downs, 0, grad_rows)
    project(pre_down.at[other], downs, 1, grad_rows)

    for i in range(both // 128):
        at = pl.ds(i * 128, 128)
        gate_value, upward, hidden_grad = pre[0, at], pre[1, at], pre_down[at]
        sigma = jax.nn.sigmoid(gate_value)
        keep(0, at, hidden_grad * upward * (sigma * (1.0 + gate_value * (1.0 - sigma))))
        keep(1, at, hidden_grad * (gate_value * sigma))

    near_in = give(part_in, [(0, gates), (1, ups)], 1)
    on_out = add_on(part_out, near_out, 0)
    swap_gate = swap_grad(0, token_rows)
    swap_up = swap_grad(1, token_rows)
    wait_sends(out_tokens[0])
    finish(part_out, on_out, sent_tokens, 0)
    home_out = all_to_all(sent_tokens, back_out)
    on_in = add_on(part_in, near_in, 1)
    writes = [own_grad(2, grad_rows, swap_down, grad_down)]

    def merge(table, arrived, parts, near, target):
        wait_sends(near)
        coarse = table.astype(BF16)
        fine = (table - coarse.astype(F32)).astype(BF16)

        def one(i):
            at = columns(i, STEP)
            total = dot(coarse, arrived[:, at]) + dot(fine, arrived[:, at])
            parts[pl.ds(0, token_count), at] = total.astype(BF16)

        over(width // STEP, one)
        return local(parts.at[pl.ds(0, token_count)], target)

    wait_sends(out_grads[0])
    finish(part_in, on_in, sent_grads, 1)
    home_in = all_to_all(sent_grads, back_in)
    landed(home_out)
    named = jnp.where(token_ids == chosen_ref[...], 1.0, 0.0).astype(F32)
    writes.append(merge(named * scale_ref[...], back_out, part_out, near_out, moe_out))
    writes.append(own_grad(0, token_rows, swap_gate, grad_gate))
    writes.append(own_grad(1, token_rows, swap_up, grad_up))
    landed(home_in)
    wait_sends(near_in)
    only = named.astype(BF16)

    def merge_grads(i):
        at = columns(i, STEP)
        part_in[pl.ds(0, token_count), at] = dot(only, back_in[:, at]).astype(BF16)

    over(width // STEP, merge_grads)
    writes.append(local(part_in.at[pl.ds(0, token_count)], grad_tokens))

    wait_sends(swaps + list(token_spread) + list(grad_spread) + list(on_out) + list(on_in))
    wait_sends([swap_down, swap_gate, swap_up] + home_out[0] + home_in[0])
    for copy in writes:
        copy.wait()


def on_device(tokens, cotangent, slot_token, slot_weight, w_gate, w_up, w_down):
    n_dp, n_expert = lax.axis_size("dp"), lax.axis_size("expert")
    slot = slot_token.shape[2]
    block = n_expert * slot
    token_count, width = tokens.shape
    shard = w_down.shape[1]
    cut = width * 3 // 5
    rest = width - cut
    gate_t = jnp.swapaxes(w_gate[0], 0, 1)
    up_t = jnp.swapaxes(w_up[0], 0, 1)
    whole = pl.BlockSpec(memory_space=pl.ANY)
    small = pl.BlockSpec(memory_space=pltpu.VMEM)
    weights = pltpu.VMEM((2 * shard, width), BF16)
    rows = pltpu.VMEM((4 * block, width), BF16)
    one = pltpu.VMEM((block, width), BF16)
    copies = 3 + 4 * (n_expert - 1) + 8 + 10 + 3
    results = pl.pallas_call(
        functools.partial(layer, (n_dp, n_expert, slot)),
        out_shape=[
            jax.ShapeDtypeStruct((token_count, width), BF16),
            jax.ShapeDtypeStruct((token_count, width), BF16),
            jax.ShapeDtypeStruct((shard, width), BF16),
            jax.ShapeDtypeStruct((shard, width), BF16),
            jax.ShapeDtypeStruct((shard, width), BF16),
        ],
        in_specs=[small, small] + [whole] * 5,
        out_specs=[whole] * 5,
        scratch_shapes=[
            weights,
            weights,
            weights,
            rows,
            rows,
            one,
            one,
            rows,
            rows,
            pltpu.VMEM((2, 2 * block, cut), BF16),
            pltpu.VMEM((2, 2 * block, rest), BF16),
            pltpu.VMEM((2, block, cut), BF16),
            pltpu.VMEM((2, block, rest), BF16),
            one,
            one,
            pltpu.VMEM((3 * shard, width), BF16),
            pltpu.VMEM((3 * shard, width), BF16),
            pltpu.VMEM((3, 2 * shard, 4 * block), BF16),
            pltpu.VMEM((3, 4 * block, 2 * shard), BF16),
            pltpu.VMEM((2, 2 * shard, 4 * block), F32),
            pltpu.VMEM((2 * shard, 4 * block), F32),
            pltpu.SemaphoreType.DMA((copies,)),
            pltpu.SemaphoreType.DMA((copies,)),
            pltpu.SemaphoreType.DMA((14,)),
        ],
        compiler_params=pltpu.CompilerParams(
            collective_id=0, has_side_effects=True, vmem_limit_bytes=67043328
        ),
        name="layer",
    )(
        slot_token.reshape(1, block),
        slot_weight.reshape(1, block),
        tokens,
        cotangent,
        gate_t,
        up_t,
        w_down[0],
    )
    moe_out, grad_tokens, grad_gate, grad_up, grad_down = results
    return (
        moe_out,
        grad_tokens,
        jnp.swapaxes(grad_gate, 0, 1)[None],
        jnp.swapaxes(grad_up, 0, 1)[None],
        grad_down[None],
    )


def solution(mesh):
    in_specs = (
        P(("dp", "expert"), None),
        P(("dp", "expert"), None),
        P(("dp", "expert"), None, None),
        P(("dp", "expert"), None, None),
        P("expert", None, "dp"),
        P("expert", None, "dp"),
        P("expert", "dp", None),
    )
    out_specs = (
        P(("dp", "expert"), None),
        P(("dp", "expert"), None),
        P("expert", None, "dp"),
        P("expert", None, "dp"),
        P("expert", "dp", None),
    )
    return jax.shard_map(
        on_device, mesh=mesh, in_specs=in_specs, out_specs=out_specs, check_vma=False
    )
```

```python
import functools

import jax
import jax.numpy as jnp
from jax import lax
from jax.experimental import pallas as pl
from jax.experimental.pallas import tpu as pltpu
from jax.sharding import PartitionSpec as P

MESH = pl.DeviceIdType.MESH
F32 = jnp.float32
BF16 = jnp.bfloat16
STEP = 512


def dot(left, right, left_dim=1, right_dim=0):
    return lax.dot_general(
        left, right, (((left_dim,), (right_dim,)), ((), ())), preferred_element_type=F32
    )


def over(count, body):
    lax.fori_loop(0, count, lambda i, carry: (body(i), carry)[1], 0)


def columns(index, width, base=0):
    return pl.ds(pl.multiple_of(base + index * width, 128), width)


def flat(table):
    slot, n_expert = table.shape
    row = lax.broadcasted_iota(jnp.int32, (slot, n_expert * slot), 0)
    lane = lax.broadcasted_iota(jnp.int32, (slot, n_expert * slot), 1)
    wide = jnp.zeros(lane.shape, table.dtype)
    for j in range(n_expert):
        wide = jnp.where(lane == j * slot + row, table[:, j : j + 1], wide)
    return jnp.sum(wide, axis=0, keepdims=True)


def names(chosen, token_count):
    block = chosen.shape[1]
    token_ids = lax.broadcasted_iota(jnp.int32, (token_count, block), 0)
    return jnp.where(token_ids == chosen, 1.0, 0.0).astype(F32)


def layer(
    sizes,
    chosen_in,
    scale_in,
    tokens,
    cotangent,
    w_gate,
    w_up,
    w_down,
    back_out,
    back_in,
    grad_gate,
    grad_up,
    grad_down,
    chosen_ref,
    scale_ref,
    gates,
    ups,
    downs,
    token_rows,
    grad_rows,
    sent_tokens,
    sent_grads,
    part_out,
    part_in,
    first_a,
    first_b,
    second_a,
    second_b,
    swap_from,
    swap_to,
    acts_t,
    acts,
    pre,
    pre_down,
    send_sems,
    recv_sems,
    local_sems,
):
    n_dp, n_expert, slot = sizes
    n_y = n_dp // 2
    d = lax.axis_index("dp")
    e = lax.axis_index("expert")
    x_hi, y = d // n_y, d % n_y
    core = e % 2
    near = (1 - 2 * core) * (1 - 2 * (y % 2))
    side_x = ((1 - x_hi) * n_y + y, e)
    side_y = (x_hi * n_y + (y - near + n_y) % n_y, e)
    side_w = (x_hi * n_y + (y + near + n_y) % n_y, e)
    peers = [(d, (e + k) % n_expert) for k in range(1, n_expert)]
    width = tokens.shape[1]
    token_count = tokens.shape[0]
    block = n_expert * slot
    all_rows = 4 * block
    shard = w_down.shape[0]
    both = 2 * shard
    cut = first_a.shape[2]
    rest = width - cut
    part_a, part_b = pl.ds(0, cut), pl.ds(cut, rest)

    counter = [0]

    def remote(source, target, device):
        i = counter[0]
        counter[0] += 1
        return pltpu.make_async_remote_copy(
            src_ref=source,
            dst_ref=target,
            send_sem=send_sems.at[i],
            recv_sem=recv_sems.at[i],
            device_id=device,
            device_id_type=MESH,
        )

    local_counter = [0]

    def local(source, target):
        i = local_counter[0]
        local_counter[0] += 1
        copy = pltpu.make_async_copy(source, target, local_sems.at[i])
        copy.start()
        return copy

    take_table = [local(chosen_in, chosen_ref), local(scale_in, scale_ref)]
    take_tokens = local(tokens, swap_from.at[pl.ds(0, token_count)])
    take_cotangent = local(cotangent, swap_from.at[pl.ds(token_count, token_count)])
    weights = ((w_gate, gates), (w_up, ups), (w_down, downs))
    take_weights = [local(own, held.at[pl.ds(0, shard)]) for own, held in weights]

    barrier = pltpu.get_barrier_semaphore()
    partners = peers + [side_x, side_y, side_w]
    for partner in partners:
        pl.semaphore_signal(barrier, inc=1, device_id=partner, device_id_type=MESH)
    pl.semaphore_wait(barrier, len(partners))

    swaps = [remote(own, held.at[pl.ds(shard, shard)], side_w) for own, held in weights]
    for copy in swaps:
        copy.start()

    def all_to_all(source, target):
        copies = [
            remote(source.at[pl.ds(peer[1] * slot, slot)], target.at[pl.ds(e * slot, slot)], peer)
            for peer in peers
        ]
        for copy in copies:
            copy.start()
        mine = local(source.at[pl.ds(e * slot, slot)], target.at[pl.ds(e * slot, slot)])
        return copies, mine

    def landed(group):
        for copy in group[0]:
            copy.wait_recv()
        group[1].wait()

    def wait_sends(copies):
        for copy in copies:
            copy.wait_send()

    for copy in take_table:
        copy.wait()
    picks = jnp.transpose(names(flat(chosen_ref[...]), token_count)).astype(BF16)
    scale_column = jnp.transpose(jnp.broadcast_to(flat(scale_ref[...]), (block, block)))[:, :1]

    take_tokens.wait()

    def pick_tokens(i):
        at = columns(i, STEP)
        sent_tokens[:, at] = dot(picks, swap_from[pl.ds(0, token_count), at]).astype(BF16)

    over(width // STEP, pick_tokens)
    out_tokens = all_to_all(sent_tokens, token_rows)
    take_cotangent.wait()

    def pick_grads(i):
        at = columns(i, STEP)
        rows = dot(picks, swap_from[pl.ds(token_count, token_count), at])
        sent_grads[:, at] = (rows * scale_column).astype(BF16)

    over(width // STEP, pick_grads)
    out_grads = all_to_all(sent_grads, grad_rows)

    def block_of(i, n=1):
        return pl.ds(i * block, n * block)

    def spread(rows):
        to_x = remote(rows.at[block_of(0)], rows.at[block_of(1)], side_x)
        to_y = remote(rows.at[block_of(0)], rows.at[block_of(2)], side_y)
        on_y = remote(rows.at[block_of(1), part_a], rows.at[block_of(3), part_a], side_y)
        on_x = remote(rows.at[block_of(2), part_b], rows.at[block_of(3), part_b], side_x)
        return to_x, to_y, on_y, on_x

    def relay(group):
        to_x, to_y, on_y, on_x = group
        to_y.wait_recv()
        on_x.start()
        to_x.wait_recv()
        on_y.start()

    landed(out_tokens)
    token_spread = spread(token_rows)
    token_spread[0].start()
    token_spread[1].start()
    relay(token_spread)
    landed(out_grads)
    grad_spread = spread(grad_rows)
    grad_spread[0].start()
    grad_spread[1].start()

    deep = 2 * STEP

    def project(target, weight, side, rows):
        target[...] = jnp.zeros(target.shape, F32)

        def one(i):
            at = columns(i, deep)
            target[...] += dot(weight[pl.ds(side * shard, shard), at], rows[:, at], 1, 1)

        over(width // deep, one)

    for copy in take_weights:
        copy.wait()
    token_spread[2].wait_recv()
    token_spread[3].wait_recv()
    own, other = pl.ds(0, shard), pl.ds(shard, shard)
    project(pre.at[0, own], gates, 0, token_rows)
    project(pre.at[1, own], ups, 0, token_rows)
    swaps[0].wait_recv()
    project(pre.at[0, other], gates, 1, token_rows)
    swaps[1].wait_recv()
    project(pre.at[1, other], ups, 1, token_rows)

    def keep(which, at, value):
        acts_t[which, at] = value.astype(BF16)
        acts[which, :, at] = jnp.transpose(value).astype(BF16)

    for i in range(both // 128):
        at = pl.ds(i * 128, 128)
        gate_value = pre[0, at]
        keep(2, at, gate_value * jax.nn.sigmoid(gate_value) * pre[1, at])

    relay(grad_spread)

    def give(parts, terms, stream):
        def one(i):
            at = columns(i, STEP)
            total = dot(acts[terms[0][0]], terms[0][1][:, at])
            for which, weight in terms[1:]:
                total += dot(acts[which], weight[:, at])
            parts[:, at] = total.astype(BF16)

        over(cut // STEP, one)
        near_y = remote(parts.at[block_of(2, 2), part_a], first_a.at[stream], side_y)
        near_y.start()
        over(rest // STEP, lambda i: one(i + cut // STEP))
        me_x = remote(parts.at[block_of(1), part_b], first_b.at[stream, block_of(0)], side_x)
        far_x = remote(parts.at[block_of(3), part_b], first_b.at[stream, block_of(1)], side_x)
        me_x.start()
        far_x.start()
        return near_y, me_x, far_x

    def add_on(parts, near, stream):
        near_y, me_x, far_x = near
        near_y.wait_recv()

        def one(i):
            at = columns(i, STEP)
            total = parts[block_of(1), at].astype(F32) + first_a[stream, block_of(1), at].astype(F32)
            first_a[stream, block_of(1), at] = total.astype(BF16)

        over(cut // STEP, one)
        on_x = remote(first_a.at[stream, block_of(1)], second_a.at[stream], side_x)
        on_x.start()
        far_x.wait_recv()

        def two(i):
            at = columns(i, STEP)
            of = columns(i, STEP, cut)
            total = parts[block_of(2), of].astype(F32) + first_b[stream, block_of(1), at].astype(F32)
            first_b[stream, block_of(1), at] = total.astype(BF16)

        over(rest // STEP, two)
        on_y = remote(first_b.at[stream, block_of(1)], second_b.at[stream], side_y)
        on_y.start()
        me_x.wait_recv()
        return on_x, on_y

    def finish(parts, on, sums, stream):
        on_x, on_y = on
        on_x.wait_recv()

        def one(i):
            at = columns(i, STEP)
            total = parts[block_of(0), at].astype(F32) + first_a[stream, block_of(0), at].astype(F32)
            sums[:, at] = (total + second_a[stream, :, at].astype(F32)).astype(BF16)

        over(cut // STEP, one)
        on_y.wait_recv()

        def two(i):
            at = columns(i, STEP)
            of = columns(i, STEP, cut)
            total = parts[block_of(0), of].astype(F32) + first_b[stream, block_of(0), at].astype(F32)
            sums[:, of] = (total + second_b[stream, :, at].astype(F32)).astype(BF16)

        over(rest // STEP, two)

    swaps[2].wait_recv()
    near_out = give(part_out, [(2, downs)], 0)

    grad_spread[2].wait_recv()
    grad_spread[3].wait_recv()

    def slab(which):
        return pl.ds(which * shard, shard)

    def swap_grad(which, rows):
        def one(i):
            at = columns(i, STEP)
            swap_from[slab(which), at] = dot(acts_t[which, other], rows[:, at]).astype(BF16)

        over(width // STEP, one)
        copy = remote(swap_from.at[slab(which)], swap_to.at[slab(which)], side_w)
        copy.start()
        return copy

    def own_grad(which, rows, copy, target):
        copy.wait_recv()

        def one(i):
            at = columns(i, STEP)
            total = dot(acts_t[which, own], rows[:, at]) + swap_to[slab(which), at].astype(F32)
            swap_to[slab(which), at] = total.astype(BF16)

        over(width // STEP, one)
        return local(swap_to.at[slab(which)], target)

    swap_down = swap_grad(2, grad_rows)
    project(pre_down.at[own], downs, 0, grad_rows)
    project(pre_down.at[other], downs, 1, grad_rows)

    for i in range(both // 128):
        at = pl.ds(i * 128, 128)
        gate_value, upward, hidden_grad = pre[0, at], pre[1, at], pre_down[at]
        sigma = jax.nn.sigmoid(gate_value)
        keep(0, at, hidden_grad * upward * (sigma * (1.0 + gate_value * (1.0 - sigma))))
        keep(1, at, hidden_grad * (gate_value * sigma))

    near_in = give(part_in, [(0, gates), (1, ups)], 1)
    on_out = add_on(part_out, near_out, 0)
    swap_gate = swap_grad(0, token_rows)
    swap_up = swap_grad(1, token_rows)
    wait_sends(out_tokens[0])
    finish(part_out, on_out, sent_tokens, 0)
    home_out = all_to_all(sent_tokens, back_out)
    on_in = add_on(part_in, near_in, 1)
    writes = [own_grad(2, grad_rows, swap_down, grad_down)]

    wait_sends(out_grads[0])
    finish(part_in, on_in, sent_grads, 1)
    home_in = all_to_all(sent_grads, back_in)
    writes.append(own_grad(0, token_rows, swap_gate, grad_gate))
    writes.append(own_grad(1, token_rows, swap_up, grad_up))
    landed(home_out)
    landed(home_in)
    wait_sends(near_out + near_in)

    wait_sends(swaps + list(token_spread) + list(grad_spread) + list(on_out) + list(on_in))
    wait_sends([swap_down, swap_gate, swap_up] + home_out[0] + home_in[0])
    for copy in writes:
        copy.wait()


PIECES = 4


def merge(
    chosen_ref,
    scale_ref,
    back_out,
    back_in,
    *refs,
):
    grads, (moe_out, grad_tokens), grads_out = refs[:3], refs[3:5], refs[5:8]
    arrived, merged, held, in_sems, out_sems = refs[8:]
    token_count, width = moe_out.shape
    deep = width // (PIECES + 1)
    tall = grads[0].shape[0] // PIECES
    reads, jobs = [], []

    def read(source, target):
        copy = pltpu.make_async_copy(source, target, in_sems.at[len(reads)])
        copy.start()
        reads.append(copy)

    for which, back in enumerate((back_out, back_in)):
        for i in range(width // deep):
            at = pl.ds(i * deep, deep)
            read(back.at[:, at], arrived.at[which, :, at])
            target = (moe_out, grad_tokens)[which].at[:, at]
            jobs.append((which, i, merged.at[which, :, at], target))
    for which, grad in enumerate(grads):
        for i in range(PIECES):
            at = pl.ds(i * tall, tall)
            read(grad.at[at], held.at[which, at])
            jobs.append((None, i, held.at[which, at], grads_out[which].at[at]))

    named = names(flat(chosen_ref[...]), token_count)
    table = named * flat(scale_ref[...])
    coarse = table.astype(BF16)
    fine = (table - coarse.astype(F32)).astype(BF16)
    only = named.astype(BF16)
    writes = []
    for n, (which, i, source, target) in enumerate(jobs):
        reads[n].wait()
        if which is not None:
            for half in range(2):
                at = pl.ds(i * deep + half * (deep // 2), deep // 2)
                rows = arrived[which, :, at]
                total = dot(only, rows) if which else dot(coarse, rows) + dot(fine, rows)
                merged[which, :, at] = total.astype(BF16)
        copy = pltpu.make_async_copy(source, target, out_sems.at[n])
        copy.start()
        writes.append(copy)
    for copy in writes:
        copy.wait()


def on_device(tokens, cotangent, slot_token, slot_weight, w_gate, w_up, w_down):
    n_dp, n_expert = lax.axis_size("dp"), lax.axis_size("expert")
    slot = slot_token.shape[2]
    block = n_expert * slot
    token_count, width = tokens.shape
    shard = w_down.shape[1]
    cut = width * 3 // 5
    rest = width - cut
    gate_t = jnp.swapaxes(w_gate[0], 0, 1)
    up_t = jnp.swapaxes(w_up[0], 0, 1)
    chosen, scale = (jnp.swapaxes(table[0], 0, 1) for table in (slot_token, slot_weight))
    whole = pl.BlockSpec(memory_space=pl.ANY)
    small = pl.BlockSpec(memory_space=pltpu.VMEM)
    weights = pltpu.VMEM((2 * shard, width), BF16)
    rows = pltpu.VMEM((4 * block, width), BF16)
    one = pltpu.VMEM((block, width), BF16)
    copies = 3 + 4 * (n_expert - 1) + 8 + 10 + 3
    results = pl.pallas_call(
        functools.partial(layer, (n_dp, n_expert, slot)),
        out_shape=[
            jax.ShapeDtypeStruct((block, width), BF16),
            jax.ShapeDtypeStruct((block, width), BF16),
            jax.ShapeDtypeStruct((shard, width), BF16),
            jax.ShapeDtypeStruct((shard, width), BF16),
            jax.ShapeDtypeStruct((shard, width), BF16),
        ],
        in_specs=[whole] * 7,
        out_specs=[whole] * 5,
        scratch_shapes=[
            pltpu.VMEM((slot, n_expert), jnp.int32),
            pltpu.VMEM((slot, n_expert), F32),
            weights,
            weights,
            weights,
            rows,
            rows,
            one,
            one,
            rows,
            rows,
            pltpu.VMEM((2, 2 * block, cut), BF16),
            pltpu.VMEM((2, 2 * block, rest), BF16),
            pltpu.VMEM((2, block, cut), BF16),
            pltpu.VMEM((2, block, rest), BF16),
            pltpu.VMEM((3 * shard, width), BF16),
            pltpu.VMEM((3 * shard, width), BF16),
            pltpu.VMEM((3, 2 * shard, 4 * block), BF16),
            pltpu.VMEM((3, 4 * block, 2 * shard), BF16),
            pltpu.VMEM((2, 2 * shard, 4 * block), F32),
            pltpu.VMEM((2 * shard, 4 * block), F32),
            pltpu.SemaphoreType.DMA((copies,)),
            pltpu.SemaphoreType.DMA((copies,)),
            pltpu.SemaphoreType.DMA((14,)),
        ],
        compiler_params=pltpu.CompilerParams(
            collective_id=0, has_side_effects=True, vmem_limit_bytes=67043328
        ),
        name="layer",
    )(
        chosen,
        scale,
        tokens,
        cotangent,
        gate_t,
        up_t,
        w_down[0],
    )
    moved = 2 * (PIECES + 1) + 3 * PIECES
    results = pl.pallas_call(
        merge,
        out_shape=[jax.ShapeDtypeStruct((token_count, width), BF16)] * 2
        + [jax.ShapeDtypeStruct((shard, width), BF16)] * 3,
        in_specs=[small] * 2 + [whole] * 5,
        out_specs=[whole] * 5,
        scratch_shapes=[
            pltpu.VMEM((2, block, width), BF16),
            pltpu.VMEM((2, token_count, width), BF16),
            pltpu.VMEM((3, shard, width), BF16),
            pltpu.SemaphoreType.DMA((moved,)),
            pltpu.SemaphoreType.DMA((moved,)),
        ],
        compiler_params=pltpu.CompilerParams(vmem_limit_bytes=67043328),
        name="merge",
    )(chosen, scale, *results)
    moe_out, grad_tokens, grad_gate, grad_up, grad_down = results
    return (
        moe_out,
        grad_tokens,
        jnp.swapaxes(grad_gate, 0, 1)[None],
        jnp.swapaxes(grad_up, 0, 1)[None],
        grad_down[None],
    )


def solution(mesh):
    in_specs = (
        P(("dp", "expert"), None),
        P(("dp", "expert"), None),
        P(("dp", "expert"), None, None),
        P(("dp", "expert"), None, None),
        P("expert", None, "dp"),
        P("expert", None, "dp"),
        P("expert", "dp", None),
    )
    out_specs = (
        P(("dp", "expert"), None),
        P(("dp", "expert"), None),
        P("expert", None, "dp"),
        P("expert", None, "dp"),
        P("expert", "dp", None),
    )
    return jax.shard_map(
        on_device, mesh=mesh, in_specs=in_specs, out_specs=out_specs, check_vma=False
    )
```

```python
import functools

import jax
import jax.numpy as jnp
from jax import lax
from jax.experimental import pallas as pl
from jax.experimental.pallas import tpu as pltpu
from jax.sharding import PartitionSpec as P

MESH = pl.DeviceIdType.MESH
F32 = jnp.float32
BF16 = jnp.bfloat16
STEP = 512


def dot(left, right, left_dim=1, right_dim=0):
    return lax.dot_general(
        left, right, (((left_dim,), (right_dim,)), ((), ())), preferred_element_type=F32
    )


def over(count, body):
    lax.fori_loop(0, count, lambda i, carry: (body(i), carry)[1], 0)


def columns(index, width, base=0):
    return pl.ds(pl.multiple_of(base + index * width, 128), width)


def flat(table):
    slot, n_expert = table.shape
    row = lax.broadcasted_iota(jnp.int32, (slot, n_expert * slot), 0)
    lane = lax.broadcasted_iota(jnp.int32, (slot, n_expert * slot), 1)
    wide = jnp.zeros(lane.shape, table.dtype)
    for j in range(n_expert):
        wide = jnp.where(lane == j * slot + row, table[:, j : j + 1], wide)
    return jnp.sum(wide, axis=0, keepdims=True)


def names(chosen, token_count):
    block = chosen.shape[1]
    token_ids = lax.broadcasted_iota(jnp.int32, (token_count, block), 0)
    return jnp.where(token_ids == chosen, 1.0, 0.0).astype(F32)


def layer(
    sizes,
    chosen_in,
    scale_in,
    tokens,
    cotangent,
    w_gate,
    w_up,
    w_down,
    back_out,
    back_in,
    far_out,
    far_in,
    grad_gate,
    grad_up,
    grad_down,
    chosen_ref,
    scale_ref,
    gates,
    ups,
    downs,
    token_rows,
    grad_rows,
    sent_tokens,
    sent_grads,
    part_out,
    part_in,
    first_a,
    first_b,
    second_b,
    swap_from,
    swap_to,
    acts_t,
    acts,
    pre,
    pre_down,
    send_sems,
    recv_sems,
    local_sems,
):
    n_dp, n_expert, slot = sizes
    n_y = n_dp // 2
    d = lax.axis_index("dp")
    e = lax.axis_index("expert")
    x_hi, y = d // n_y, d % n_y
    core = e % 2
    near = (1 - 2 * core) * (1 - 2 * (y % 2))
    side_x = ((1 - x_hi) * n_y + y, e)
    side_y = (x_hi * n_y + (y - near + n_y) % n_y, e)
    side_w = (x_hi * n_y + (y + near + n_y) % n_y, e)
    peers = [(d, (e + k) % n_expert) for k in range(1, n_expert)]
    far_peers = [(side_x[0], (e + k) % n_expert) for k in range(n_expert)]
    width = tokens.shape[1]
    token_count = tokens.shape[0]
    block = n_expert * slot
    all_rows = 4 * block
    shard = w_down.shape[0]
    both = 2 * shard
    cut = first_a.shape[2]
    rest = width - cut
    part_a, part_b = pl.ds(0, cut), pl.ds(cut, rest)

    counter = [0]

    def remote(source, target, device):
        i = counter[0]
        counter[0] += 1
        return pltpu.make_async_remote_copy(
            src_ref=source,
            dst_ref=target,
            send_sem=send_sems.at[i],
            recv_sem=recv_sems.at[i],
            device_id=device,
            device_id_type=MESH,
        )

    local_counter = [0]

    def local(source, target):
        i = local_counter[0]
        local_counter[0] += 1
        copy = pltpu.make_async_copy(source, target, local_sems.at[i])
        copy.start()
        return copy

    take_table = [local(chosen_in, chosen_ref), local(scale_in, scale_ref)]
    take_tokens = local(tokens, swap_from.at[pl.ds(0, token_count)])
    take_cotangent = local(cotangent, swap_from.at[pl.ds(token_count, token_count)])
    weights = ((w_gate, gates), (w_up, ups), (w_down, downs))
    take_weights = [local(own, held.at[pl.ds(0, shard)]) for own, held in weights]

    barrier = pltpu.get_barrier_semaphore()
    partners = peers + far_peers + [side_y, side_w]
    for partner in partners:
        pl.semaphore_signal(barrier, inc=1, device_id=partner, device_id_type=MESH)
    pl.semaphore_wait(barrier, len(partners))

    swaps = [remote(own, held.at[pl.ds(shard, shard)], side_w) for own, held in weights]
    for copy in swaps:
        copy.start()

    def all_to_all(source, target, to=peers):
        copies = [
            remote(source.at[pl.ds(peer[1] * slot, slot)], target.at[pl.ds(e * slot, slot)], peer)
            for peer in to
        ]
        for copy in copies:
            copy.start()
        if to is far_peers:
            return copies, None
        mine = local(source.at[pl.ds(e * slot, slot)], target.at[pl.ds(e * slot, slot)])
        return copies, mine

    def landed(group):
        for copy in group[0]:
            copy.wait_recv()
        if group[1] is not None:
            group[1].wait()

    def wait_sends(copies):
        for copy in copies:
            copy.wait_send()

    for copy in take_table:
        copy.wait()
    picks = jnp.transpose(names(flat(chosen_ref[...]), token_count)).astype(BF16)
    scale_column = jnp.transpose(jnp.broadcast_to(flat(scale_ref[...]), (block, block)))[:, :1]

    def block_of(i, n=1):
        return pl.ds(i * block, n * block)

    def deal(sent, rows):
        near_group = all_to_all(sent, rows.at[block_of(0)])
        far_from, far_to = sent.at[:, part_a], rows.at[block_of(1), part_a]
        return near_group, all_to_all(far_from, far_to, far_peers)

    take_tokens.wait()

    def pick_tokens(i):
        at = columns(i, STEP)
        sent_tokens[:, at] = dot(picks, swap_from[pl.ds(0, token_count), at]).astype(BF16)

    over(width // STEP, pick_tokens)
    out_tokens = deal(sent_tokens, token_rows)
    take_cotangent.wait()

    def pick_grads(i):
        at = columns(i, STEP)
        rows = dot(picks, swap_from[pl.ds(token_count, token_count), at])
        sent_grads[:, at] = (rows * scale_column).astype(BF16)

    over(width // STEP, pick_grads)
    out_grads = deal(sent_grads, grad_rows)

    def spread(rows, dealt):
        to_y_b = remote(rows.at[block_of(0), part_b], rows.at[block_of(2), part_b], side_y)
        to_y_a = remote(rows.at[block_of(0), part_a], rows.at[block_of(2), part_a], side_y)
        to_x = remote(rows.at[block_of(0), part_b], rows.at[block_of(1), part_b], side_x)
        on_y = remote(rows.at[block_of(1), part_a], rows.at[block_of(3), part_a], side_y)
        on_x = remote(rows.at[block_of(2), part_b], rows.at[block_of(3), part_b], side_x)
        landed(dealt[0])
        to_y_b.start()
        to_y_a.start()
        to_x.start()
        landed(dealt[1])
        on_y.start()
        return to_y_b, to_y_a, to_x, on_y, on_x

    def relay(group):
        group[0].wait_recv()
        group[4].start()

    token_spread = spread(token_rows, out_tokens)
    relay(token_spread)
    grad_spread = spread(grad_rows, out_grads)

    deep = 2 * STEP

    def project(target, weight, side, rows):
        target[...] = jnp.zeros(target.shape, F32)

        def one(i):
            at = columns(i, deep)
            target[...] += dot(weight[pl.ds(side * shard, shard), at], rows[:, at], 1, 1)

        over(width // deep, one)

    for copy in take_weights:
        copy.wait()
    for copy in token_spread[1:]:
        copy.wait_recv()
    own, other = pl.ds(0, shard), pl.ds(shard, shard)
    project(pre.at[0, own], gates, 0, token_rows)
    project(pre.at[1, own], ups, 0, token_rows)
    swaps[0].wait_recv()
    project(pre.at[0, other], gates, 1, token_rows)
    swaps[1].wait_recv()
    project(pre.at[1, other], ups, 1, token_rows)

    def keep(which, at, value):
        acts_t[which, at] = value.astype(BF16)
        acts[which, :, at] = jnp.transpose(value).astype(BF16)

    for i in range(both // 128):
        at = pl.ds(i * 128, 128)
        gate_value = pre[0, at]
        keep(2, at, gate_value * jax.nn.sigmoid(gate_value) * pre[1, at])

    relay(grad_spread)

    def give(parts, terms, stream):
        def one(i):
            at = columns(i, STEP)
            total = dot(acts[terms[0][0]], terms[0][1][:, at])
            for which, weight in terms[1:]:
                total += dot(acts[which], weight[:, at])
            parts[:, at] = total.astype(BF16)

        over(cut // STEP, one)
        near_y = remote(parts.at[block_of(2, 2), part_a], first_a.at[stream], side_y)
        near_y.start()
        over(rest // STEP, lambda i: one(i + cut // STEP))
        me_x = remote(parts.at[block_of(1), part_b], first_b.at[stream, block_of(0)], side_x)
        far_x = remote(parts.at[block_of(3), part_b], first_b.at[stream, block_of(1)], side_x)
        me_x.start()
        far_x.start()
        return near_y, me_x, far_x

    def add_on(parts, near, back, far, stream):
        near_y, me_x, far_x = near
        near_y.wait_recv()

        def one(i):
            at = columns(i, STEP)
            total = parts[block_of(0, 2), at].astype(F32) + first_a[stream, :, at].astype(F32)
            first_a[stream, :, at] = total.astype(BF16)

        over(cut // STEP, one)
        summed = first_a.at[stream]
        away = all_to_all(summed.at[block_of(1)], far, far_peers)
        home = all_to_all(summed.at[block_of(0)], back.at[:, part_a])
        far_x.wait_recv()

        def two(i):
            at = columns(i, STEP)
            of = columns(i, STEP, cut)
            total = parts[block_of(2), of].astype(F32) + first_b[stream, block_of(1), at].astype(F32)
            first_b[stream, block_of(1), at] = total.astype(BF16)

        over(rest // STEP, two)
        on_y = remote(first_b.at[stream, block_of(1)], second_b.at[stream], side_y)
        on_y.start()
        me_x.wait_recv()
        return on_y, [away, home]

    def finish(parts, on_y, sums, back, stream):
        on_y.wait_recv()

        def two(i):
            at = columns(i, STEP)
            of = columns(i, STEP, cut)
            total = parts[block_of(0), of].astype(F32) + first_b[stream, block_of(0), at].astype(F32)
            sums[:, of] = (total + second_b[stream, :, at].astype(F32)).astype(BF16)

        over(rest // STEP, two)
        return all_to_all(sums.at[:, part_b], back.at[:, part_b])

    swaps[2].wait_recv()
    near_out = give(part_out, [(2, downs)], 0)

    for copy in grad_spread[1:]:
        copy.wait_recv()

    def slab(which):
        return pl.ds(which * shard, shard)

    def swap_grad(which, rows):
        def one(i):
            at = columns(i, STEP)
            swap_from[slab(which), at] = dot(acts_t[which, other], rows[:, at]).astype(BF16)

        over(width // STEP, one)
        copy = remote(swap_from.at[slab(which)], swap_to.at[slab(which)], side_w)
        copy.start()
        return copy

    def own_grad(which, rows, copy, target):
        copy.wait_recv()

        def one(i):
            at = columns(i, STEP)
            total = dot(acts_t[which, own], rows[:, at]) + swap_to[slab(which), at].astype(F32)
            swap_to[slab(which), at] = total.astype(BF16)

        over(width // STEP, one)
        return local(swap_to.at[slab(which)], target)

    swap_down = swap_grad(2, grad_rows)
    project(pre_down.at[own], downs, 0, grad_rows)
    project(pre_down.at[other], downs, 1, grad_rows)

    for i in range(both // 128):
        at = pl.ds(i * 128, 128)
        gate_value, upward, hidden_grad = pre[0, at], pre[1, at], pre_down[at]
        sigma = jax.nn.sigmoid(gate_value)
        keep(0, at, hidden_grad * upward * (sigma * (1.0 + gate_value * (1.0 - sigma))))
        keep(1, at, hidden_grad * (gate_value * sigma))

    near_in = give(part_in, [(0, gates), (1, ups)], 1)
    on_out, homes = add_on(part_out, near_out, back_out, far_out, 0)
    swap_gate = swap_grad(0, token_rows)
    swap_up = swap_grad(1, token_rows)
    for group in out_tokens + out_grads:
        wait_sends(group[0])
    homes.append(finish(part_out, on_out, sent_tokens, back_out, 0))
    on_in, more = add_on(part_in, near_in, back_in, far_in, 1)
    homes += more
    writes = [own_grad(2, grad_rows, swap_down, grad_down)]
    homes.append(finish(part_in, on_in, sent_grads, back_in, 1))
    writes.append(own_grad(0, token_rows, swap_gate, grad_gate))
    writes.append(own_grad(1, token_rows, swap_up, grad_up))
    for group in homes:
        landed(group)
        wait_sends(group[0])
    wait_sends(near_out + near_in)
    wait_sends(swaps + list(token_spread) + list(grad_spread) + [on_out, on_in])
    wait_sends([swap_down, swap_gate, swap_up])
    for copy in writes:
        copy.wait()


PIECES = 4


def merge(
    chosen_ref,
    scale_ref,
    back_out,
    back_in,
    far_out,
    far_in,
    *refs,
):
    grads, (moe_out, grad_tokens), grads_out = refs[:3], refs[3:5], refs[5:8]
    arrived, arrived_far, merged, held, in_sems, out_sems = refs[8:]
    token_count, width = moe_out.shape
    cut = far_out.shape[1]
    tall = grads[0].shape[0] // PIECES
    reads, jobs = [], []

    def read(source, target):
        copy = pltpu.make_async_copy(source, target, in_sems.at[len(reads)])
        copy.start()
        reads.append(copy)
        return copy

    for which, back, far in ((0, back_out, far_out), (1, back_in, far_in)):
        for i in range(width // STEP):
            at = pl.ds(i * STEP, STEP)
            wait = [read(back.at[:, at], arrived.at[which, :, at])]
            if i * STEP < cut:
                wait.append(read(far.at[:, at], arrived_far.at[which, :, at]))
            target = (moe_out, grad_tokens)[which].at[:, at]
            jobs.append((wait, which, at, merged.at[which, :, at], target))
    for which, grad in enumerate(grads):
        for i in range(PIECES):
            at = pl.ds(i * tall, tall)
            wait = [read(grad.at[at], held.at[which, at])]
            jobs.append((wait, None, at, held.at[which, at], grads_out[which].at[at]))

    named = names(flat(chosen_ref[...]), token_count)
    table = named * flat(scale_ref[...])
    coarse = table.astype(BF16)
    fine = (table - coarse.astype(F32)).astype(BF16)
    only = named.astype(BF16)
    writes = []
    for n, (wait, which, at, source, target) in enumerate(jobs):
        for copy in wait:
            copy.wait()
        if which is not None:
            total = jnp.zeros((token_count, STEP), F32)
            for held_rows in (arrived, arrived_far)[: len(wait)]:
                rows = held_rows[which, :, at]
                total += dot(only, rows) if which else dot(coarse, rows) + dot(fine, rows)
            merged[which, :, at] = total.astype(BF16)
        copy = pltpu.make_async_copy(source, target, out_sems.at[n])
        copy.start()
        writes.append(copy)
    for copy in writes:
        copy.wait()


def on_device(tokens, cotangent, slot_token, slot_weight, w_gate, w_up, w_down):
    n_dp, n_expert = lax.axis_size("dp"), lax.axis_size("expert")
    slot = slot_token.shape[2]
    block = n_expert * slot
    token_count, width = tokens.shape
    shard = w_down.shape[1]
    cut = width // 2
    rest = width - cut
    gate_t = jnp.swapaxes(w_gate[0], 0, 1)
    up_t = jnp.swapaxes(w_up[0], 0, 1)
    chosen, scale = (jnp.swapaxes(table[0], 0, 1) for table in (slot_token, slot_weight))
    whole = pl.BlockSpec(memory_space=pl.ANY)
    small = pl.BlockSpec(memory_space=pltpu.VMEM)
    weights = pltpu.VMEM((2 * shard, width), BF16)
    rows = pltpu.VMEM((4 * block, width), BF16)
    one = pltpu.VMEM((block, width), BF16)
    near_copies, far_copies = n_expert - 1, n_expert
    copies = 3 + 2 * (near_copies + far_copies + 5 + 4 + 2 * near_copies + far_copies) + 3
    results = pl.pallas_call(
        functools.partial(layer, (n_dp, n_expert, slot)),
        out_shape=[
            jax.ShapeDtypeStruct((block, width), BF16),
            jax.ShapeDtypeStruct((block, width), BF16),
            jax.ShapeDtypeStruct((block, cut), BF16),
            jax.ShapeDtypeStruct((block, cut), BF16),
            jax.ShapeDtypeStruct((shard, width), BF16),
            jax.ShapeDtypeStruct((shard, width), BF16),
            jax.ShapeDtypeStruct((shard, width), BF16),
        ],
        in_specs=[whole] * 7,
        out_specs=[whole] * 7,
        scratch_shapes=[
            pltpu.VMEM((slot, n_expert), jnp.int32),
            pltpu.VMEM((slot, n_expert), F32),
            weights,
            weights,
            weights,
            rows,
            rows,
            one,
            one,
            rows,
            rows,
            pltpu.VMEM((2, 2 * block, cut), BF16),
            pltpu.VMEM((2, 2 * block, rest), BF16),
            pltpu.VMEM((2, block, rest), BF16),
            pltpu.VMEM((3 * shard, width), BF16),
            pltpu.VMEM((3 * shard, width), BF16),
            pltpu.VMEM((3, 2 * shard, 4 * block), BF16),
            pltpu.VMEM((3, 4 * block, 2 * shard), BF16),
            pltpu.VMEM((2, 2 * shard, 4 * block), F32),
            pltpu.VMEM((2 * shard, 4 * block), F32),
            pltpu.SemaphoreType.DMA((copies,)),
            pltpu.SemaphoreType.DMA((copies,)),
            pltpu.SemaphoreType.DMA((16,)),
        ],
        compiler_params=pltpu.CompilerParams(
            collective_id=0, has_side_effects=True, vmem_limit_bytes=67043328
        ),
        name="layer",
    )(
        chosen,
        scale,
        tokens,
        cotangent,
        gate_t,
        up_t,
        w_down[0],
    )
    stored = 2 * (width // STEP) + 3 * PIECES
    taken = stored + 2 * (cut // STEP)
    results = pl.pallas_call(
        merge,
        out_shape=[jax.ShapeDtypeStruct((token_count, width), BF16)] * 2
        + [jax.ShapeDtypeStruct((shard, width), BF16)] * 3,
        in_specs=[small] * 2 + [whole] * 7,
        out_specs=[whole] * 5,
        scratch_shapes=[
            pltpu.VMEM((2, block, width), BF16),
            pltpu.VMEM((2, block, cut), BF16),
            pltpu.VMEM((2, token_count, width), BF16),
            pltpu.VMEM((3, shard, width), BF16),
            pltpu.SemaphoreType.DMA((taken,)),
            pltpu.SemaphoreType.DMA((stored,)),
        ],
        compiler_params=pltpu.CompilerParams(vmem_limit_bytes=67043328),
        name="merge",
    )(chosen, scale, *results)
    moe_out, grad_tokens, grad_gate, grad_up, grad_down = results
    return (
        moe_out,
        grad_tokens,
        jnp.swapaxes(grad_gate, 0, 1)[None],
        jnp.swapaxes(grad_up, 0, 1)[None],
        grad_down[None],
    )


def solution(mesh):
    in_specs = (
        P(("dp", "expert"), None),
        P(("dp", "expert"), None),
        P(("dp", "expert"), None, None),
        P(("dp", "expert"), None, None),
        P("expert", None, "dp"),
        P("expert", None, "dp"),
        P("expert", "dp", None),
    )
    out_specs = (
        P(("dp", "expert"), None),
        P(("dp", "expert"), None),
        P("expert", None, "dp"),
        P("expert", None, "dp"),
        P("expert", "dp", None),
    )
    return jax.shard_map(
        on_device, mesh=mesh, in_specs=in_specs, out_specs=out_specs, check_vma=False
    )
```

```python
import functools

import jax
import jax.numpy as jnp
from jax import lax
from jax.experimental import pallas as pl
from jax.experimental.pallas import tpu as pltpu
from jax.sharding import PartitionSpec as P

MESH = pl.DeviceIdType.MESH
F32 = jnp.float32
BF16 = jnp.bfloat16
STEP = 512


def dot(left, right, left_dim=1, right_dim=0):
    return lax.dot_general(
        left, right, (((left_dim,), (right_dim,)), ((), ())), preferred_element_type=F32
    )


def over(count, body):
    lax.fori_loop(0, count, lambda i, carry: (body(i), carry)[1], 0)


def columns(index, width, base=0):
    return pl.ds(pl.multiple_of(base + index * width, 128), width)


def flat(table):
    slot, n_expert = table.shape
    row = lax.broadcasted_iota(jnp.int32, (slot, n_expert * slot), 0)
    lane = lax.broadcasted_iota(jnp.int32, (slot, n_expert * slot), 1)
    wide = jnp.zeros(lane.shape, table.dtype)
    for j in range(n_expert):
        wide = jnp.where(lane == j * slot + row, table[:, j : j + 1], wide)
    return jnp.sum(wide, axis=0, keepdims=True)


def names(chosen, token_count):
    block = chosen.shape[1]
    token_ids = lax.broadcasted_iota(jnp.int32, (token_count, block), 0)
    return jnp.where(token_ids == chosen, 1.0, 0.0).astype(F32)


def layer(
    sizes,
    chosen_in,
    scale_in,
    tokens,
    cotangent,
    w_gate,
    w_up,
    w_down,
    back_out,
    back_in,
    far_out,
    far_in,
    grad_gate,
    grad_up,
    grad_down,
    chosen_ref,
    scale_ref,
    gates,
    ups,
    downs,
    token_rows,
    grad_rows,
    sent_tokens,
    sent_grads,
    part_out,
    part_in,
    first_a,
    first_b,
    second_b,
    swap_from,
    swap_to,
    acts_t,
    acts,
    pre,
    pre_down,
    send_sems,
    recv_sems,
    local_sems,
):
    n_dp, n_expert, slot = sizes
    n_y = n_dp // 2
    d = lax.axis_index("dp")
    e = lax.axis_index("expert")
    x_hi, y = d // n_y, d % n_y
    core = e % 2
    near = (1 - 2 * core) * (1 - 2 * (y % 2))
    side_x = ((1 - x_hi) * n_y + y, e)
    side_y = (x_hi * n_y + (y - near + n_y) % n_y, e)
    side_w = (x_hi * n_y + (y + near + n_y) % n_y, e)
    peers = [(d, (e + k) % n_expert) for k in range(1, n_expert)]
    far_peers = [(side_x[0], (e + k) % n_expert) for k in range(n_expert)]
    width = tokens.shape[1]
    token_count = tokens.shape[0]
    block = n_expert * slot
    all_rows = 4 * block
    shard = w_down.shape[0]
    both = 2 * shard
    cut = first_a.shape[2]
    rest = width - cut
    part_a, part_b = pl.ds(0, cut), pl.ds(cut, rest)

    counter = [0]

    def remote(source, target, device):
        i = counter[0]
        counter[0] += 1
        return pltpu.make_async_remote_copy(
            src_ref=source,
            dst_ref=target,
            send_sem=send_sems.at[i],
            recv_sem=recv_sems.at[i],
            device_id=device,
            device_id_type=MESH,
        )

    local_counter = [0]

    def local(source, target):
        i = local_counter[0]
        local_counter[0] += 1
        copy = pltpu.make_async_copy(source, target, local_sems.at[i])
        copy.start()
        return copy

    take_table = [local(chosen_in, chosen_ref), local(scale_in, scale_ref)]
    take_tokens = local(tokens, swap_from.at[pl.ds(0, token_count)])
    take_cotangent = local(cotangent, swap_from.at[pl.ds(token_count, token_count)])
    weights = ((w_gate, gates), (w_up, ups), (w_down, downs))
    take_weights = [local(own, held.at[pl.ds(0, shard)]) for own, held in weights]

    barrier = pltpu.get_barrier_semaphore()
    partners = peers + far_peers + [side_y, side_w]
    for partner in partners:
        pl.semaphore_signal(barrier, inc=1, device_id=partner, device_id_type=MESH)
    pl.semaphore_wait(barrier, len(partners))

    swaps = [remote(own, held.at[pl.ds(shard, shard)], side_w) for own, held in weights]
    for copy in swaps:
        copy.start()

    def all_to_all(source, target, to=peers):
        copies = [
            remote(source.at[pl.ds(peer[1] * slot, slot)], target.at[pl.ds(e * slot, slot)], peer)
            for peer in to
        ]
        for copy in copies:
            copy.start()
        if to is far_peers:
            return copies, None
        mine = local(source.at[pl.ds(e * slot, slot)], target.at[pl.ds(e * slot, slot)])
        return copies, mine

    def landed(group):
        for copy in group[0]:
            copy.wait_recv()
        if group[1] is not None:
            group[1].wait()

    def wait_sends(copies):
        for copy in copies:
            copy.wait_send()

    for copy in take_table:
        copy.wait()
    picks = jnp.transpose(names(flat(chosen_ref[...]), token_count)).astype(BF16)
    scale_column = jnp.transpose(jnp.broadcast_to(flat(scale_ref[...]), (block, block)))[:, :1]

    def block_of(i, n=1):
        return pl.ds(i * block, n * block)

    def deal(sent, rows):
        near_group = all_to_all(sent, rows.at[block_of(0)])
        far_from, far_to = sent.at[:, part_a], rows.at[block_of(1), part_a]
        return near_group, all_to_all(far_from, far_to, far_peers)

    take_tokens.wait()

    def pick_tokens(i):
        at = columns(i, STEP)
        sent_tokens[:, at] = dot(picks, swap_from[pl.ds(0, token_count), at]).astype(BF16)

    over(width // STEP, pick_tokens)
    out_tokens = deal(sent_tokens, token_rows)
    take_cotangent.wait()

    def pick_grads(i):
        at = columns(i, STEP)
        rows = dot(picks, swap_from[pl.ds(token_count, token_count), at])
        sent_grads[:, at] = (rows * scale_column).astype(BF16)

    over(width // STEP, pick_grads)
    out_grads = deal(sent_grads, grad_rows)

    def spread(rows, dealt):
        to_y_b = remote(rows.at[block_of(0), part_b], rows.at[block_of(2), part_b], side_y)
        to_y_a = remote(rows.at[block_of(0), part_a], rows.at[block_of(2), part_a], side_y)
        to_x = remote(rows.at[block_of(0), part_b], rows.at[block_of(1), part_b], side_x)
        on_y = remote(rows.at[block_of(1), part_a], rows.at[block_of(3), part_a], side_y)
        on_x = remote(rows.at[block_of(2), part_b], rows.at[block_of(3), part_b], side_x)
        landed(dealt[0])
        to_y_b.start()
        to_y_a.start()
        to_x.start()
        landed(dealt[1])
        on_y.start()
        return to_y_b, to_y_a, to_x, on_y, on_x

    def relay(group):
        group[0].wait_recv()
        group[4].start()

    token_spread = spread(token_rows, out_tokens)
    relay(token_spread)
    grad_spread = spread(grad_rows, out_grads)

    deep = 2 * STEP

    def project(target, weight, side, rows):
        target[...] = jnp.zeros(target.shape, F32)

        def one(i):
            at = columns(i, deep)
            target[...] += dot(weight[pl.ds(side * shard, shard), at], rows[:, at], 1, 1)

        over(width // deep, one)

    for copy in take_weights:
        copy.wait()
    for copy in token_spread[1:]:
        copy.wait_recv()
    own, other = pl.ds(0, shard), pl.ds(shard, shard)
    project(pre.at[0, own], gates, 0, token_rows)
    project(pre.at[1, own], ups, 0, token_rows)
    swaps[0].wait_recv()
    project(pre.at[0, other], gates, 1, token_rows)
    swaps[1].wait_recv()
    project(pre.at[1, other], ups, 1, token_rows)

    def keep(which, at, value):
        acts_t[which, at] = value.astype(BF16)
        acts[which, :, at] = jnp.transpose(value).astype(BF16)

    for i in range(both // 128):
        at = pl.ds(i * 128, 128)
        gate_value = pre[0, at]
        keep(2, at, gate_value * jax.nn.sigmoid(gate_value) * pre[1, at])

    relay(grad_spread)

    def give(parts, terms, stream):
        def one(i):
            at = columns(i, STEP)
            total = dot(acts[terms[0][0]], terms[0][1][:, at])
            for which, weight in terms[1:]:
                total += dot(acts[which], weight[:, at])
            parts[:, at] = total.astype(BF16)

        over(cut // STEP, one)
        near_y = remote(parts.at[block_of(2, 2), part_a], first_a.at[stream], side_y)
        near_y.start()
        over(rest // STEP, lambda i: one(i + cut // STEP))
        me_x = remote(parts.at[block_of(1), part_b], first_b.at[stream, block_of(0)], side_x)
        far_x = remote(parts.at[block_of(3), part_b], first_b.at[stream, block_of(1)], side_x)
        me_x.start()
        far_x.start()
        return near_y, me_x, far_x

    def add_on(parts, near, back, far, stream):
        near_y, me_x, far_x = near
        near_y.wait_recv()

        def one(i):
            at = columns(i, STEP)
            total = parts[block_of(0, 2), at].astype(F32) + first_a[stream, :, at].astype(F32)
            first_a[stream, :, at] = total.astype(BF16)

        over(cut // STEP, one)
        summed = first_a.at[stream]
        away = all_to_all(summed.at[block_of(1)], far, far_peers)
        home = all_to_all(summed.at[block_of(0)], back.at[:, part_a])
        far_x.wait_recv()

        def two(i):
            at = columns(i, STEP)
            of = columns(i, STEP, cut)
            total = parts[block_of(2), of].astype(F32) + first_b[stream, block_of(1), at].astype(F32)
            first_b[stream, block_of(1), at] = total.astype(BF16)

        over(rest // STEP, two)
        on_y = remote(first_b.at[stream, block_of(1)], second_b.at[stream], side_y)
        on_y.start()
        me_x.wait_recv()
        return on_y, [away, home]

    def finish(parts, on_y, sums, back, stream):
        on_y.wait_recv()

        def two(i):
            at = columns(i, STEP)
            of = columns(i, STEP, cut)
            total = parts[block_of(0), of].astype(F32) + first_b[stream, block_of(0), at].astype(F32)
            sums[:, of] = (total + second_b[stream, :, at].astype(F32)).astype(BF16)

        over(rest // STEP, two)
        return all_to_all(sums.at[:, part_b], back.at[:, part_b])

    swaps[2].wait_recv()
    near_out = give(part_out, [(2, downs)], 0)

    for copy in grad_spread[1:]:
        copy.wait_recv()

    def slab(which):
        return pl.ds(which * shard, shard)

    def swap_grad(which, rows):
        def one(i):
            at = columns(i, STEP)
            swap_from[slab(which), at] = dot(acts_t[which, other], rows[:, at]).astype(BF16)

        over(width // STEP, one)
        copy = remote(swap_from.at[slab(which)], swap_to.at[slab(which)], side_w)
        copy.start()
        return copy

    def own_grad(which, rows, copy, target):
        copy.wait_recv()

        def one(i):
            at = columns(i, STEP)
            total = dot(acts_t[which, own], rows[:, at]) + swap_to[slab(which), at].astype(F32)
            swap_to[slab(which), at] = total.astype(BF16)

        over(width // STEP, one)
        return local(swap_to.at[slab(which)], target)

    swap_down = swap_grad(2, grad_rows)
    project(pre_down.at[own], downs, 0, grad_rows)
    project(pre_down.at[other], downs, 1, grad_rows)

    for i in range(both // 128):
        at = pl.ds(i * 128, 128)
        gate_value, upward, hidden_grad = pre[0, at], pre[1, at], pre_down[at]
        sigma = jax.nn.sigmoid(gate_value)
        keep(0, at, hidden_grad * upward * (sigma * (1.0 + gate_value * (1.0 - sigma))))
        keep(1, at, hidden_grad * (gate_value * sigma))

    near_in = give(part_in, [(0, gates), (1, ups)], 1)
    on_out, homes = add_on(part_out, near_out, back_out, far_out, 0)
    swap_gate = swap_grad(0, token_rows)
    swap_up = swap_grad(1, token_rows)
    for group in out_tokens + out_grads:
        wait_sends(group[0])
    homes.append(finish(part_out, on_out, sent_tokens, back_out, 0))
    on_in, more = add_on(part_in, near_in, back_in, far_in, 1)
    homes += more
    writes = [own_grad(2, grad_rows, swap_down, grad_down)]
    homes.append(finish(part_in, on_in, sent_grads, back_in, 1))
    writes.append(own_grad(0, token_rows, swap_gate, grad_gate))
    writes.append(own_grad(1, token_rows, swap_up, grad_up))
    for group in homes:
        landed(group)
        wait_sends(group[0])
    wait_sends(near_out + near_in)
    wait_sends(swaps + list(token_spread) + list(grad_spread) + [on_out, on_in])
    wait_sends([swap_down, swap_gate, swap_up])
    for copy in writes:
        copy.wait()


PIECES = 4
PIECE = 1280


def merge(
    chosen_ref,
    scale_ref,
    back_out,
    back_in,
    far_out,
    far_in,
    *refs,
):
    grads, (moe_out, grad_tokens), grads_out = refs[:3], refs[3:5], refs[5:8]
    arrived, merged, held, in_sems, out_sems = refs[8:]
    token_count, width = moe_out.shape
    block, cut = far_out.shape
    tall = grads[0].shape[0] // PIECES
    reads, jobs = [], []

    def read(source, target):
        copy = pltpu.make_async_copy(source, target, in_sems.at[len(reads)])
        copy.start()
        reads.append(copy)
        return copy

    for which, back, far in ((0, back_out, far_out), (1, back_in, far_in)):
        for i in range(width // PIECE):
            at = pl.ds(i * PIECE, PIECE)
            wait = [read(back.at[:, at], arrived.at[which, pl.ds(0, block), at])]
            if i * PIECE < cut:
                wait.append(read(far.at[:, at], arrived.at[which, pl.ds(block, block), at]))
            target = (moe_out, grad_tokens)[which].at[:, at]
            jobs.append((wait, which, i, merged.at[which, :, at], target))
    for which, grad in enumerate(grads):
        for i in range(PIECES):
            at = pl.ds(i * tall, tall)
            wait = [read(grad.at[at], held.at[which, at])]
            jobs.append((wait, None, i, held.at[which, at], grads_out[which].at[at]))

    named = names(flat(chosen_ref[...]), token_count)
    named = jnp.concatenate([named, named], axis=1)
    scale = flat(scale_ref[...])
    table = named * jnp.concatenate([scale, scale], axis=1)
    coarse = table.astype(BF16)
    fine = (table - coarse.astype(F32)).astype(BF16)
    only = named.astype(BF16)
    writes = []
    for n, (wait, which, i, source, target) in enumerate(jobs):
        for copy in wait:
            copy.wait()
        if which is not None:
            deep = len(wait) * block
            for k in range(PIECE // 256):
                at = pl.ds(i * PIECE + k * 256, 256)
                rows = arrived[which, pl.ds(0, deep), at]
                if which:
                    total = dot(only[:, :deep], rows)
                else:
                    total = dot(coarse[:, :deep], rows) + dot(fine[:, :deep], rows)
                merged[which, :, at] = total.astype(BF16)
        copy = pltpu.make_async_copy(source, target, out_sems.at[n])
        copy.start()
        writes.append(copy)
    for copy in writes:
        copy.wait()


def on_device(tokens, cotangent, slot_token, slot_weight, w_gate, w_up, w_down):
    n_dp, n_expert = lax.axis_size("dp"), lax.axis_size("expert")
    slot = slot_token.shape[2]
    block = n_expert * slot
    token_count, width = tokens.shape
    shard = w_down.shape[1]
    cut = width // 2
    rest = width - cut
    gate_t = jnp.swapaxes(w_gate[0], 0, 1)
    up_t = jnp.swapaxes(w_up[0], 0, 1)
    chosen, scale = (jnp.swapaxes(table[0], 0, 1) for table in (slot_token, slot_weight))
    whole = pl.BlockSpec(memory_space=pl.ANY)
    small = pl.BlockSpec(memory_space=pltpu.VMEM)
    weights = pltpu.VMEM((2 * shard, width), BF16)
    rows = pltpu.VMEM((4 * block, width), BF16)
    one = pltpu.VMEM((block, width), BF16)
    near_copies, far_copies = n_expert - 1, n_expert
    copies = 3 + 2 * (near_copies + far_copies + 5 + 4 + 2 * near_copies + far_copies) + 3
    results = pl.pallas_call(
        functools.partial(layer, (n_dp, n_expert, slot)),
        out_shape=[
            jax.ShapeDtypeStruct((block, width), BF16),
            jax.ShapeDtypeStruct((block, width), BF16),
            jax.ShapeDtypeStruct((block, cut), BF16),
            jax.ShapeDtypeStruct((block, cut), BF16),
            jax.ShapeDtypeStruct((shard, width), BF16),
            jax.ShapeDtypeStruct((shard, width), BF16),
            jax.ShapeDtypeStruct((shard, width), BF16),
        ],
        in_specs=[whole] * 7,
        out_specs=[whole] * 7,
        scratch_shapes=[
            pltpu.VMEM((slot, n_expert), jnp.int32),
            pltpu.VMEM((slot, n_expert), F32),
            weights,
            weights,
            weights,
            rows,
            rows,
            one,
            one,
            rows,
            rows,
            pltpu.VMEM((2, 2 * block, cut), BF16),
            pltpu.VMEM((2, 2 * block, rest), BF16),
            pltpu.VMEM((2, block, rest), BF16),
            pltpu.VMEM((3 * shard, width), BF16),
            pltpu.VMEM((3 * shard, width), BF16),
            pltpu.VMEM((3, 2 * shard, 4 * block), BF16),
            pltpu.VMEM((3, 4 * block, 2 * shard), BF16),
            pltpu.VMEM((2, 2 * shard, 4 * block), F32),
            pltpu.VMEM((2 * shard, 4 * block), F32),
            pltpu.SemaphoreType.DMA((copies,)),
            pltpu.SemaphoreType.DMA((copies,)),
            pltpu.SemaphoreType.DMA((16,)),
        ],
        compiler_params=pltpu.CompilerParams(
            collective_id=0, has_side_effects=True, vmem_limit_bytes=67043328
        ),
        name="layer",
    )(
        chosen,
        scale,
        tokens,
        cotangent,
        gate_t,
        up_t,
        w_down[0],
    )
    stored = 2 * (width // PIECE) + 3 * PIECES
    taken = stored + 2 * (cut // PIECE)
    results = pl.pallas_call(
        merge,
        out_shape=[jax.ShapeDtypeStruct((token_count, width), BF16)] * 2
        + [jax.ShapeDtypeStruct((shard, width), BF16)] * 3,
        in_specs=[small] * 2 + [whole] * 7,
        out_specs=[whole] * 5,
        scratch_shapes=[
            pltpu.VMEM((2, 2 * block, width), BF16),
            pltpu.VMEM((2, token_count, width), BF16),
            pltpu.VMEM((3, shard, width), BF16),
            pltpu.SemaphoreType.DMA((taken,)),
            pltpu.SemaphoreType.DMA((stored,)),
        ],
        compiler_params=pltpu.CompilerParams(vmem_limit_bytes=67043328),
        name="merge",
    )(chosen, scale, *results)
    moe_out, grad_tokens, grad_gate, grad_up, grad_down = results
    return (
        moe_out,
        grad_tokens,
        jnp.swapaxes(grad_gate, 0, 1)[None],
        jnp.swapaxes(grad_up, 0, 1)[None],
        grad_down[None],
    )


def solution(mesh):
    in_specs = (
        P(("dp", "expert"), None),
        P(("dp", "expert"), None),
        P(("dp", "expert"), None, None),
        P(("dp", "expert"), None, None),
        P("expert", None, "dp"),
        P("expert", None, "dp"),
        P("expert", "dp", None),
    )
    out_specs = (
        P(("dp", "expert"), None),
        P(("dp", "expert"), None),
        P("expert", None, "dp"),
        P("expert", None, "dp"),
        P("expert", "dp", None),
    )
    return jax.shard_map(
        on_device, mesh=mesh, in_specs=in_specs, out_specs=out_specs, check_vma=False
    )
```
